256 devices in a mesh: row: 32 (over z, y), col: 8 (over x, core).
Axes of the slice: x: 4, y: 4, z: 8, core: 2. Of those that a mesh axis runs over, the one named last changes fastest.
Arguments:
- density_values: float32 [8192, 1024], P('row', 'col'), may hold values from -5 to 5
- density_cols: int32 [128, 16], P('row', 'col'), may hold values from 0 to 127, as said below
- ks_cols: int32 [128, 32], P('row', 'col'), may hold values from 0 to 127, as said below
- core_hamiltonian: float32 [8192, 2048], P('row', 'col'), may hold values from -3 to 3
- tile_blocks: int32 [256, 16], P('row'), may hold values from 0 to 127, as said below
- grid_weights: float32 [256, 128], P('row'), may hold values from 0.5 to 2
- basis_values: float32 [256, 128, 1024], P('row'), may hold values from -1.5 to 1.5
Outputs:
- kohn_sham: float32 [8192, 2048], P('row', 'col')
- purified: float32 [8192, 1024], P('row', 'col')
The draws below stay inside these ranges and needn't reach their ends.
Inputs may be any that keep to these rules, and one draw needn't show every extreme that they name: `density_cols`: for each block row and each index c of col, the 2 entries in slots c * 2 .. c * 2 + 1 are different block columns of c * 16 .. c * 16 + 15. `ks_cols`: for each block row and each index c of col, the 4 entries in slots c * 4 .. c * 4 + 3 are different block columns of c * 16 .. c * 16 + 15. `tile_blocks`: each tile names 16 different blocks.
All inputs are finite; a program needn't handle non-finite values.
Results may differ from the reference program's by a relative error of at most 0.0003.
Values sent between devices are 32-bit elements; how exact they have to be, the bound alone decides.
No kernel may reach another device: no remote copies, remote signals or barrier semaphores. Data moves between devices by JAX's collectives and lax.ppermute only.
A program may use at most 128 MiB of HBM per device.

```python
import math
import jax
import jax.numpy as jnp
from jax import lax

BS = 64
TB = 16
G = 128
NZR = 2
NZK = 4
NB = 128
BC_DEV = 16
N = 8192
SLOTS = 16
KSLOTS = 32
TILES = 256
N_COL = 8


def chosen_offsets(key, rows, span, keep):
    scores = jax.random.randint(key, (rows, span), 0, 1048576)
    distinct = scores * span + jnp.arange(span, dtype=jnp.int32)[None, :]
    ordering = jnp.argsort(distinct, axis=1)
    ranking = jnp.argsort(ordering, axis=1)
    chosen = (ranking < keep).astype(jnp.int32)
    slots = jnp.cumsum(chosen, axis=1) - 1
    picked = (chosen[:, None, :] == 1) & (slots[:, None, :] == jnp.arange(keep, dtype=jnp.int32)[None, :, None])
    return jnp.sum(jnp.where(picked, jnp.arange(span, dtype=jnp.int32)[None, None, :], 0), axis=2).astype(jnp.int32)


def band_columns(key, keep):
    groups = NB // BC_DEV
    span = 2 * keep
    offsets = chosen_offsets(key, NB * groups, span, keep).reshape(NB, groups, keep) - keep
    centre = jnp.arange(NB, dtype=jnp.int32) % BC_DEV
    local_ids = (centre[:, None, None] + offsets + BC_DEV) % BC_DEV
    columns = jnp.arange(groups, dtype=jnp.int32)[None, :, None] * BC_DEV + local_ids
    return columns.reshape(NB, groups * keep).astype(jnp.int32)


def draw_density_cols(key, part):
    return band_columns(jax.random.fold_in(key, 11), NZR)


def draw_ks_cols(key, part):
    return band_columns(jax.random.fold_in(key, 23), NZK)


def draw_tile_blocks(key, part):
    key_start, key_pick = jax.random.split(jax.random.fold_in(key, 41), 2)
    groups = NB // BC_DEV
    starts = jax.random.randint(key_start, (TILES,), 0, NB)
    offsets = chosen_offsets(key_pick, TILES, 2 * TB, TB)
    spatial = (starts[:, None] + offsets) % NB
    return (spatial % groups * BC_DEV + spatial // groups).astype(jnp.int32)


def draw_density_values(key, part):
    key_entries, key_rows, key_cols = jax.random.split(jax.random.fold_in(key, 37), 3)
    width = NB // BC_DEV * NZR * BS
    row_place = jnp.arange(N, dtype=jnp.float32) / N
    trend = jnp.exp(row_place * math.log(3.0))
    entries = jnp.clip(jax.random.normal(key_entries, (N, width), jnp.float32), -4.0, 4.0)
    row_scale = trend * jnp.exp(math.log(10.0) * jax.random.uniform(key_rows, (N,), jnp.float32))
    col_scale = jnp.exp(math.log(4.0) * jax.random.uniform(key_cols, (width,), jnp.float32))
    return 0.01 * entries * row_scale[:, None] * col_scale[None, :]


def level_of(rng, shape, shards, smallest, largest):
    def one(axis_at, shards_of):
        steps = jax.random.uniform(jax.random.fold_in(jax.random.fold_in(rng, 6), axis_at), (shards_of,), jnp.float32, smallest / len(shards), largest / len(shards))
        return jnp.repeat(jnp.exp(steps), shape[axis_at] // shards_of).reshape((-1,) + (1,) * (len(shape) - axis_at - 1))

    level = one(*shards[0])
    for cut in shards[1:]:
        level = level * one(*cut)
    return level


def bell_draw(own_key, shape, deviation, limit, cuts=(), kind=jnp.bfloat16):
    array = jax.random.normal(own_key, shape, jnp.float32) * deviation
    if len(cuts) > 0:
        array = level_of(own_key, shape, cuts, -0.22, 0.18) * array
    return jnp.clip(array, min=-limit, max=limit).astype(kind)


def setup_inputs(seed: int = 0) -> dict:
    seeds = jax.random.split(jax.random.key(seed), 8)
    return {
        "density_values": draw_density_values(jax.random.fold_in(seeds[7], 71), 0),
        "density_cols": draw_density_cols(jax.random.fold_in(seeds[7], 71), 0),
        "ks_cols": draw_ks_cols(jax.random.fold_in(seeds[7], 71), 0),
        "core_hamiltonian": bell_draw(seeds[3], (N, KSLOTS * BS), 0.5, 3.0, ((0, 32), (1, 8)), jnp.float32),
        "tile_blocks": draw_tile_blocks(jax.random.fold_in(seeds[7], 71), 0),
        "grid_weights": jnp.clip(jnp.exp(math.log(2.0) - 1.3862944 * jax.random.uniform(seeds[5], (TILES, G), jnp.float32) ** level_of(seeds[5], (TILES, G), ((0, 32),), -0.2, 0.2)), 0.5, 2.0),
        "basis_values": bell_draw(seeds[6], (TILES, G, TB * BS), 0.25, 1.5, ((0, 32),), jnp.float32),
    }


def reference(density_values, density_cols, ks_cols, core_hamiltonian, tile_blocks, grid_weights, basis_values):
    highest = lax.Precision.HIGHEST
    dense_blocks = density_values.reshape(NB, BS, SLOTS, BS)

    def product_row(item):
        rows_here, cols_here = item
        neighbours = dense_blocks[cols_here].reshape(SLOTS, BS, N_COL, NZR, BS)
        their_cols = density_cols[cols_here].reshape(SLOTS, N_COL, NZR)
        matches = (their_cols[:, :, :, None] == cols_here.reshape(N_COL, NZR)[None, :, None, :]).astype(jnp.float32)
        combined = jnp.einsum('pcqr,pacqh->pcrah', matches, neighbours, precision=highest)
        return jnp.einsum('fpa,pcrah->fcrh', rows_here, combined, precision=highest).reshape(BS, SLOTS * BS)
    kept = lax.map(product_row, (dense_blocks, density_cols)).reshape(N, SLOTS * BS)
    mean_square = jnp.sum(kept * kept) / (N * SLOTS * BS)
    purified = kept / jnp.sqrt(mean_square + 1e-06)
    basis = basis_values.reshape(TILES, G, TB, BS)

    def tile_density(item):
        tile_ids, tile_basis = item
        rows_here = dense_blocks[tile_ids]
        cols_here = density_cols[tile_ids]
        halves = jnp.einsum('gif,ifsh->gish', tile_basis, rows_here, precision=highest)
        matches = (cols_here[:, :, None] == tile_ids[None, None, :]).astype(jnp.float32)
        combined = jnp.einsum('isj,gish->gjh', matches, halves, precision=highest)
        return lax.optimization_barrier(jnp.sum(combined * tile_basis, axis=(1, 2)))
    grid_density = lax.map(tile_density, (tile_blocks, basis))
    potential = grid_weights * jnp.tanh(grid_density)

    def add_tile(accumulated, item):
        tile_ids, tile_basis, tile_potential = item
        kept_cols = ks_cols[tile_ids]
        matches = (kept_cols[:, :, None] == tile_ids[None, None, :]).astype(jnp.float32)
        selected = jnp.einsum('isj,gjh->gish', matches, tile_basis, precision=highest)
        weighted = tile_basis * tile_potential[:, None, None]
        pairs = jnp.einsum('gif,gish->ifsh', weighted, selected, precision=highest)
        return (accumulated.at[tile_ids].add(pairs), None)
    start_sum = jnp.zeros((NB, BS, KSLOTS, BS), jnp.float32)
    accumulated, unused = lax.scan(add_tile, start_sum, (tile_blocks, basis, potential))
    kohn_sham = core_hamiltonian + accumulated.reshape(N, KSLOTS * BS)
    return (kohn_sham, purified)
```

```python
import functools
import jax
import jax.numpy as jnp
from jax import lax
from jax.experimental import pallas as pl
from jax.experimental.pallas import tpu as pltpu
from jax.sharding import PartitionSpec as P

BS = 64
TB = 16
G = 128
NY = 4
NZ = 8
PR = 264
BF = jnp.bfloat16
F32 = jnp.float32


def shift_z(x, d):
    return lax.ppermute(
        x, "row", [(z * NY + y, (z + d) % NZ * NY + y) for z in range(NZ) for y in range(NY)]
    )


def shift_y(x, d):
    return lax.ppermute(
        x, "row", [(z * NY + y, z * NY + (y + d) % NY) for z in range(NZ) for y in range(NY)]
    )


def shift_x(x, d):
    return lax.ppermute(
        x, "col", [(2 * a + b, (a + d) % 4 * 2 + b) for a in range(4) for b in range(2)]
    )


def swap_core(x):
    return lax.ppermute(x, "col", [(i, i ^ 1) for i in range(8)])


def after(x, *deps):
    return lax.optimization_barrier((x,) + deps)[0]


def split(x):
    hi = x.astype(BF)
    lo = (x - hi.astype(F32)).astype(BF)
    return hi, lo


def dot(a, b):
    return lax.dot_general(a, b, (((1,), (0,)), ((), ())), preferred_element_type=F32)


def prep_kernel(b_ref, o_ref):
    for k in range(TB // 2):
        hi, lo = split(b_ref[0, :, k * 128 : (k + 1) * 128].T)
        o_ref[0, k * 128 : (k + 1) * 128, 0:128] = hi
        o_ref[0, k * 128 : (k + 1) * 128, 128:256] = lo


def prep(basis):
    n = basis.shape[0]
    return pl.pallas_call(
        prep_kernel,
        grid=(n,),
        in_specs=[pl.BlockSpec((1, G, TB * BS), lambda t: (t, 0, 0))],
        out_specs=pl.BlockSpec((1, TB * BS, 2 * G), lambda t: (t, 0, 0)),
        out_shape=jax.ShapeDtypeStruct((n, TB * BS, 2 * G), BF),
        cost_estimate=pl.CostEstimate(flops=0, bytes_accessed=8 << 20, transcendentals=0),
        name="prep",
    )(basis)


def load_panel(pieces, panel, sem):
    rows = NY * PR
    copies = [
        pltpu.make_async_copy(p, panel.at[pl.ds(k * rows, rows)], sem.at[k])
        for k, p in enumerate(pieces)
    ]
    for c in copies:
        c.start()
    for c in copies:
        c.wait()


def grid_kernel(base_ref, jsel_ref, basis_ref, *refs):
    pieces, (rho_ref, panel, dup, acc, sem) = refs[:NZ], refs[NZ:]
    load_panel(pieces, panel, sem)
    lane = lax.broadcasted_iota(jnp.int32, (G, 128), 1)
    low = lane < BS
    dup[TB] = jnp.zeros((G, 128), F32)

    def tile(t, carry):
        for k in range(TB // 2):
            x = basis_ref[t, :, k * 128 : (k + 1) * 128]
            r = pltpu.roll(x, BS, 1)
            dup[2 * k] = jnp.where(low, x, r)
            dup[2 * k + 1] = jnp.where(low, r, x)
        total = jnp.zeros((G, 128), F32)
        zero = jnp.zeros((BS, 128), BF)
        for k in range(TB // 2):
            bhi, blo = split(basis_ref[t, :, k * 128 : (k + 1) * 128])
            d0 = panel[pl.ds(pl.multiple_of(base_ref[t * TB + 2 * k], 8), BS), :]
            d1 = panel[pl.ds(pl.multiple_of(base_ref[t * TB + 2 * k + 1], 8), BS), :]
            h0, l0 = split(d0)
            h1, l1 = split(d1)

            def diag(a, b):
                return jnp.concatenate(
                    [jnp.concatenate([a, zero], 1), jnp.concatenate([zero, b], 1)], 0
                )

            whi = diag(h0, h1)
            out = dot(jnp.concatenate([bhi, blo], 1), jnp.concatenate([whi, whi], 0))
            out = out + dot(bhi, diag(l0, l1))
            for h in range(2):
                at = (t * TB + 2 * k + h) * 2
                other = jnp.where(low, dup[jsel_ref[at]], dup[jsel_ref[at + 1]])
                total = total + out[:, h * 128 : (h + 1) * 128] * other
        acc[t] = total
        return carry

    lax.fori_loop(0, basis_ref.shape[0], tile, 0)
    for t in range(basis_ref.shape[0]):
        rho_ref[t : t + 1, :] = jnp.sum(acc[t].T, axis=0, keepdims=True)


def grid_part(base, jsel, basis, pieces):
    n = basis.shape[0]
    whole = pl.BlockSpec(memory_space=pltpu.VMEM)
    return pl.pallas_call(
        grid_kernel,
        grid_spec=pltpu.PrefetchScalarGridSpec(
            num_scalar_prefetch=2,
            grid=(1,),
            in_specs=[whole] + [pl.BlockSpec(memory_space=pl.ANY)] * NZ,
            out_specs=whole,
            scratch_shapes=[
                pltpu.VMEM((NZ * NY * PR, 128), F32),
                pltpu.VMEM((TB + 1, G, 128), F32),
                pltpu.VMEM((n, G, 128), F32),
                pltpu.SemaphoreType.DMA((NZ,)),
            ],
        ),
        out_shape=jax.ShapeDtypeStruct((n, G), F32),
        cost_estimate=pl.CostEstimate(
            flops=2 << 30, bytes_accessed=9 << 20, transcendentals=0
        ),
        name="grid_density",
    )(base, jsel, basis, *pieces)


def pairs_kernel(dst_ref, mine_ref, pot_ref, basis_ref, bt_ref, out_ref, potcol):
    n = basis_ref.shape[0]
    lane = lax.broadcasted_iota(jnp.int32, (G, 128), 1)
    low = lane < BS
    half = lax.broadcasted_iota(jnp.int32, (BS, 128), 1) // BS

    def clear(k, carry):
        out_ref[pl.ds(k * 8, 8)] = jnp.zeros((8, BS, 128), F32)
        return carry

    lax.fori_loop(0, out_ref.shape[0] // 8, clear, 0)
    pot_t = jnp.concatenate([pot_ref[...], jnp.zeros((128 - n, G), F32)], 0).T
    for t in range(n):
        potcol[t] = jnp.broadcast_to(pot_t[:, t : t + 1], (G, 128))

    def step(at, carry):
        t = at // TB
        j = at % TB

        @pl.when(mine_ref[at] == 1)
        def _():
            x = basis_ref[t, :, pl.ds(pl.multiple_of(j // 2 * 128, 128), 128)]
            r = pltpu.roll(x, BS, 1)
            even = jnp.where(low, x, r)
            odd = jnp.where(low, r, x)
            hi, lo = split(jnp.where(j % 2 == 0, even, odd) * potcol[t])
            top = jnp.concatenate([hi, lo], 1)
            both = dot(bt_ref[t], jnp.concatenate([top, top], 0))
            product = both[:, :128] + both[:, 128:]
            for i in range(TB):
                d = dst_ref[at * TB + i]
                block = product[i * BS : (i + 1) * BS]
                out_ref[d // 4] += jnp.where(half == d % 4, block, 0.0)

        return carry

    lax.fori_loop(0, n * TB, step, 0)


def pair_part(dst, mine, pot, basis, bt, blocks):
    n = basis.shape[0]
    whole = pl.BlockSpec(memory_space=pltpu.VMEM)
    return pl.pallas_call(
        pairs_kernel,
        grid_spec=pltpu.PrefetchScalarGridSpec(
            num_scalar_prefetch=2,
            grid=(1,),
            in_specs=[whole] * 3,
            out_specs=whole,
            scratch_shapes=[pltpu.VMEM((n, G, 128), F32)],
        ),
        out_shape=jax.ShapeDtypeStruct((2 * blocks, BS, 128), F32),
        cost_estimate=pl.CostEstimate(
            flops=9 << 30, bytes_accessed=16 << 20, transcendentals=0
        ),
        name="pairs",
    )(dst, mine, pot, basis, bt)


def purify_kernel(base_ref, code_ref, *refs):
    pieces, lefts, (kept_ref, square_ref, panel, sem) = refs[:NZ], refs[NZ : NZ + 4], refs[NZ + 4 :]
    load_panel(pieces, panel, sem)
    slot = lax.broadcasted_iota(jnp.int32, (BS, 128), 1) // BS
    square = jnp.zeros((BS, 128), F32)
    rows = kept_ref.shape[0] // BS
    for i in range(rows):
        total = jnp.zeros((BS, 128), F32)
        for p in range(4):
            right = []
            for s in range(4):
                at = i * 16 + p * 4 + s
                d = panel[pl.ds(pl.multiple_of(base_ref[at], 8), BS), :]
                straight = jnp.where(
                    slot == 0, code_ref[at * 4], code_ref[at * 4 + 3]
                )
                crossed = jnp.where(
                    slot == 0, code_ref[at * 4 + 2], code_ref[at * 4 + 1]
                )
                right.append(
                    jnp.where(straight == 1, d, 0.0)
                    + jnp.where(crossed == 1, pltpu.roll(d, BS, 1), 0.0)
                )
            rhi, rlo = split(jnp.concatenate(right, 0))
            left = jnp.concatenate(
                [
                    lefts[p][pl.ds(i * BS, BS), :],
                    lefts[p][pl.ds(PR + i * BS, BS), :],
                ],
                1,
            )
            lhi, llo = split(left)
            total = total + dot(lhi, rhi) + (dot(lhi, rlo) + dot(llo, rhi))
        kept_ref[pl.ds(i * BS, BS), :] = total
        square = square + total * total
    square_ref[...] = jnp.sum(square.reshape(8, 8, 128), axis=0)


def purify(base, code, pieces, lefts, rows):
    whole = pl.BlockSpec(memory_space=pltpu.VMEM)
    return pl.pallas_call(
        purify_kernel,
        grid_spec=pltpu.PrefetchScalarGridSpec(
            num_scalar_prefetch=2,
            grid=(1,),
            in_specs=[pl.BlockSpec(memory_space=pl.ANY)] * NZ + [whole] * 4,
            out_specs=[whole, whole],
            scratch_shapes=[
                pltpu.VMEM((NZ * NY * PR, 128), F32),
                pltpu.SemaphoreType.DMA((NZ,)),
            ],
        ),
        out_shape=[
            jax.ShapeDtypeStruct((rows, 128), F32),
            jax.ShapeDtypeStruct((8, 128), F32),
        ],
        cost_estimate=pl.CostEstimate(
            flops=1 << 28, bytes_accessed=6 << 20, transcendentals=0
        ),
        name="purify",
    )(base, code, *pieces, *lefts)


def gather_row(payload):
    near = [payload, shift_y(payload, 1), shift_y(payload, 2), shift_y(payload, 3)]
    own = jnp.concatenate(near, 0)
    pieces = [own] + [None] * 7
    up, down = own, own
    for k in range(1, 4):
        up, down = shift_z(up, 1), shift_z(down, 7)
        pieces[k], pieces[8 - k] = up, down
    h = NY * PR // 2
    pieces[4] = jnp.concatenate([shift_z(up[:h], 1), shift_z(down[h:], 7)], 0)
    return pieces, near


def scatter_z_ring(chunk):
    c4 = chunk(4)
    h = c4.shape[0] // 2
    up, down = shift_z(c4[:h], 1), shift_z(c4[h:], 7)
    c3, c5 = chunk(3), chunk(5)
    up = jnp.concatenate([c3[:h] + up, c3[h:]], 0)
    down = jnp.concatenate([c5[:h], c5[h:] + down], 0)
    for k in (2, 1):
        up, down = shift_z(up, 1) + chunk(k), shift_z(down, 7) + chunk(8 - k)
    return chunk(0) + (shift_z(up, 1) + shift_z(down, 7))


def scatter_y_ring(chunk):
    c2 = chunk(2)
    h = c2.shape[0] // 2
    up, down = shift_y(c2[:h], 1), shift_y(c2[h:], 3)
    c1, c3 = chunk(1), chunk(3)
    up = jnp.concatenate([c1[:h] + up, c1[h:]], 0)
    down = jnp.concatenate([c3[:h], c3[h:] + down], 0)
    return chunk(0) + (shift_y(up, 1) + shift_y(down, 3))


def on_device(
    density_values, density_cols, ks_cols, core_hamiltonian, tile_blocks, grid_weights, basis_values
):
    rows = density_values.shape[0]
    own_blocks, own_slots = density_cols.shape
    ks_slots = ks_cols.shape[1]
    blocks = own_blocks * NZ * NY
    per_col = blocks // 8
    me = lax.axis_index("row")
    z, y = me // NY, me % NY
    c = lax.axis_index("col")

    index = jnp.concatenate([density_cols.reshape(-1), ks_cols.reshape(-1)]).astype(F32)
    width = index.shape[0]
    index = jnp.pad(index[None, :], ((0, PR - rows - 1), (0, 128 - width)))
    payload = jnp.concatenate([density_values, index], 0)

    pieces, near = gather_row(payload)

    seed = after(payload, near[1], near[2], near[3])
    two = jnp.concatenate([seed, swap_core(seed)], 0)
    lefts = [two] + [shift_x(two, d) for d in (1, 2, 3)]
    bt = prep(after(basis_values, near[1], near[2], near[3]))

    table = jnp.concatenate(
        [p.reshape(NY, PR, 128)[:, rows, :width] for p in pieces], 0
    ).astype(jnp.int32)
    n_d = own_blocks * own_slots
    panel_cols = table[:, :n_d].reshape(blocks, own_slots)
    panel_ks = table[:, n_d:].reshape(blocks, ks_slots)

    def relative(b):
        r, q = b // own_blocks, b % own_blocks
        dz, dy = (z - r // NY) % NZ, (y - r % NY) % NY
        return dz, dy, q

    def row_of(b):
        dz, dy, q = relative(b)
        return (dz * NY + dy) * PR + q * BS

    def entry_of(b):
        dz, dy, q = relative(b)
        return (dz * NY + dy) * own_blocks + q

    tiles = tile_blocks.shape[0]
    entry = entry_of(tile_blocks)
    positions = jnp.arange(TB, dtype=jnp.int32)
    same = panel_cols[entry][:, :, :, None] == tile_blocks[:, None, None, :]
    jsel = jnp.min(jnp.where(same, positions, TB), axis=3)
    rho = grid_part(
        row_of(tile_blocks).reshape(-1), jsel.reshape(-1), basis_values, pieces
    )

    rho = rho + swap_core(rho)
    rho = (rho + shift_x(rho, 1)) + (shift_x(rho, 2) + shift_x(rho, 3))
    pot = grid_weights * jnp.tanh(rho)

    dz, dy, q = relative(tile_blocks)
    up_z, up_y = (NZ - dz) % NZ, (NY - dy) % NY
    place_a = (up_z * NY + up_y) * own_blocks + q
    place_b = blocks + (up_y * NZ + up_z) * own_blocks + q
    same = panel_ks[entry][:, None, :, :] == tile_blocks[:, :, None, None]
    slots = jnp.arange(ks_slots, dtype=jnp.int32)
    code = jnp.where(
        slots < 2, place_a[:, None, :, None] * 4 + slots, place_b[:, None, :, None] * 4 + slots - 2
    )
    dst = jnp.min(jnp.where(same, code, 1 << 20), axis=3)
    dst = jnp.where(dst == 1 << 20, 2, dst)
    mine = (tile_blocks // per_col == c).astype(jnp.int32)
    sums = pair_part(dst.reshape(-1), mine.reshape(-1), pot, basis_values, bt, blocks)

    left_cols = jnp.stack(
        [t.reshape(2, PR, 128)[:, rows, :n_d] for t in lefts], 0
    ).astype(jnp.int32)
    left_cols = left_cols.reshape(4, 2, own_blocks, own_slots).transpose(2, 0, 1, 3)
    theirs = panel_cols[entry_of(left_cols)]
    hit = theirs[..., :, None] == density_cols[:, None, None, None, None, :]
    kept, square = purify(
        row_of(left_cols).reshape(-1),
        hit.astype(jnp.int32).reshape(-1),
        pieces,
        lefts,
        rows,
    )
    square = jnp.sum(square).reshape(1, 1) + jnp.zeros((8, 128), F32)
    square = square + swap_core(square)
    square = (square + shift_x(square, 1)) + (shift_x(square, 2) + shift_x(square, 3))
    square = (square + shift_y(square, 1)) + (shift_y(square, 2) + shift_y(square, 3))
    for d in (1, 2, 4):
        square = square + shift_z(square, d)
    count = blocks * BS * own_slots * 8 * BS
    purified = kept / jnp.sqrt(square[0, 0] / count + 1e-06)

    na, nb = blocks // NZ, blocks // NY
    sum_a = scatter_z_ring(lambda k: sums[k * na : (k + 1) * na])
    sum_b = scatter_y_ring(lambda k: sums[blocks + k * nb : blocks + (k + 1) * nb])
    part = [sum_a[k * own_blocks : (k + 1) * own_blocks] for k in range(NY)]
    sum_a = (part[0] + shift_y(part[1], 1)) + (shift_y(part[2], 2) + shift_y(part[3], 3))
    sum_b = scatter_z_ring(lambda k: sum_b_chunk(sum_b, k, own_blocks))
    added = jnp.concatenate([sum_a.reshape(rows, 128), sum_b.reshape(rows, 128)], 1)
    kohn_sham = core_hamiltonian + added
    return (kohn_sham, purified)


def sum_b_chunk(x, k, n):
    return x[k * n : (k + 1) * n]


def solution(mesh):
    in_specs = (
        P("row", "col"),
        P("row", "col"),
        P("row", "col"),
        P("row", "col"),
        P("row", None),
        P("row", None),
        P("row", None, None),
    )
    out_specs = (P("row", "col"), P("row", "col"))
    return jax.shard_map(
        on_device, mesh=mesh, in_specs=in_specs, out_specs=out_specs, check_vma=False
    )
```
